32 devices in a mesh: col: 16 (over z, x, core), orb: 2 (over y).
Axes of the slice: x: 2, y: 2, z: 4, core: 2. Of those that a mesh axis runs over, the one named last changes fastest.
Arguments:
- slab_occ: bfloat16 [1024, 400], P('col', 'orb'), may hold values from -6 to 6
- slab_vir: bfloat16 [1024, 2400], P('col', 'orb'), may hold values from -6 to 6
- orbitals_occ: bfloat16 [400, 16384], P('orb', 'col'), may hold values from -0.3125 to 0.3125
- orbitals_vir: bfloat16 [2400, 16384], P('orb', 'col'), may hold values from -0.125 to 0.125
- occ_energy: float32 [400], P('orb'), may hold values from -2 to -0.1
- vir_energy: float32 [2400], P('orb'), may hold values from 0.1 to 3
- screened: bfloat16 [1024, 16384], P('col'), may hold values from -6 to 6
Outputs:
- occ_kernel: bfloat16 [1024, 400], P(('col', 'orb'))
- vir_kernel: bfloat16 [1024, 2400], P(('col', 'orb'))
The draws below stay inside these ranges and needn't reach their ends.
All inputs are finite; a program needn't handle non-finite values.
Results may differ from the reference program's by a relative error of at most 0.014.
Values may be sent and summed in bfloat16 or wider, within the bound.
A program may use at most 64 MiB of HBM per device.

```python
import jax
import jax.numpy as jnp
from jax import lax

NO = 400
NV = 2400
ROWS = 1024
COL_DEV = 1024
NR = 16384


def with_spikes(result, own_key, source, target, parts, factor):
    owner, partner = [(jnp.arange(result.shape[position]) // (result.shape[position] // parts)).reshape([-1 if axis == position else 1 for axis in range(result.ndim)]) for position in (source, target)]
    chosen = jax.random.permutation(own_key, parts)[partner]
    strong = (owner == chosen) | (owner == (partner + parts // 2) % parts)
    return jnp.where(strong, factor * result, result)


def levels(key, shape, split, smallest, high):
    level, own = 1.0, jax.random.fold_in(key, 6)
    for position, blocks in split:
        heights = jnp.exp(jax.random.uniform(jax.random.fold_in(own, position), (blocks,), jnp.float32, smallest / len(split), high / len(split)))
        level = level * jnp.repeat(heights, shape[position] // blocks).reshape([-1 if axis == position else 1 for axis in range(len(shape))])
    return level


def gaussian(key, extent, deviation, most, split=(), kind=jnp.bfloat16):
    entries = jax.random.normal(key, extent, jnp.float32) * deviation
    if len(split) > 0:
        entries = levels(key, extent, split, -0.22, 0.18) * entries
    return jnp.clip(entries, min=-most, max=most).astype(kind)


def bell_draw_with(rng, extent, scale, reach, split, heavy, kind=jnp.bfloat16):
    result = scale * jax.random.normal(rng, extent, jnp.float32)
    if split:
        result = result * levels(rng, extent, split, -0.22, 0.18)
    return jnp.clip(with_spikes(result, jax.random.fold_in(rng, 3), *heavy), -reach, reach).astype(kind)


def setup_inputs(seed: int = 0) -> dict:
    keys = jax.random.split(jax.random.key(seed), 8)
    return {
        "slab_occ": gaussian(keys[0], (ROWS, NO), 1.0, 6.0, ((0, 16), (1, 2))),
        "slab_vir": gaussian(keys[1], (ROWS, NV), 1.0, 6.0, ((0, 16), (1, 2))),
        "orbitals_occ": gaussian(keys[2], (NO, NR), NO ** -0.5, 0.3125, ((0, 2), (1, 16))),
        "orbitals_vir": gaussian(keys[3], (NV, NR), NV ** -0.5, 0.125, ((0, 2), (1, 16))),
        "occ_energy": jnp.clip(-2.0 + 1.9 * jax.random.uniform(keys[4], (NO,), jnp.float32) ** levels(keys[4], (NO,), ((0, 2),), -0.2, 0.2), -2.0, -0.1),
        "vir_energy": jnp.clip(0.1 + 2.9 * jax.random.uniform(keys[5], (NV,), jnp.float32) ** levels(keys[5], (NV,), ((0, 2),), -0.2, 0.2), 0.1, 3.0),
        "screened": bell_draw_with(keys[6], (ROWS, NR), (80 / NR ** 0.5), 6.0, ((0, 16),), (1, 0, 16, 2.0)),
    }


def reference(slab_occ, slab_vir, orbitals_occ, orbitals_vir, occ_energy, vir_energy, screened):
    scaled_occ = (slab_occ.astype(jnp.float32) * jnp.exp(occ_energy)[None, :]).astype(jnp.bfloat16)
    scaled_vir = (slab_vir.astype(jnp.float32) * jnp.exp(-vir_energy)[None, :]).astype(jnp.bfloat16)
    width = COL_DEV
    count = NR // width

    def advance(carry, index):
        acc_occ, acc_vir = carry
        start = (index * width).astype(jnp.int32)
        occ_cols = lax.dynamic_slice_in_dim(orbitals_occ, start, width, 1)
        vir_cols = lax.dynamic_slice_in_dim(orbitals_vir, start, width, 1)
        screen = lax.dynamic_slice_in_dim(screened, start, width, 1).astype(jnp.float32)
        green_occ = jnp.dot(scaled_occ, occ_cols, preferred_element_type=jnp.float32)
        green_vir = jnp.dot(scaled_vir, vir_cols, preferred_element_type=jnp.float32)
        occ_side = (green_vir * screen).astype(jnp.bfloat16)
        vir_side = (green_occ * screen).astype(jnp.bfloat16)
        dims = (((1,), (1,)), ((), ()))
        acc_occ = acc_occ + lax.dot_general(occ_side, occ_cols, dims, preferred_element_type=jnp.float32)
        acc_vir = acc_vir + lax.dot_general(vir_side, vir_cols, dims, preferred_element_type=jnp.float32)
        return (acc_occ, acc_vir), None

    init = (jnp.zeros((ROWS, NO), jnp.float32), jnp.zeros((ROWS, NV), jnp.float32))
    (acc_occ, acc_vir), unused = lax.scan(advance, init, jnp.arange(count, dtype=jnp.int32))
    return acc_occ.astype(jnp.bfloat16), acc_vir.astype(jnp.bfloat16)
```

```python
import functools

import jax
import jax.numpy as jnp
from jax import lax
from jax.experimental import pallas as pl
from jax.experimental.pallas import tpu as pltpu
from jax.sharding import PartitionSpec as P

MESH = pl.DeviceIdType.MESH
ANY = pl.BlockSpec(memory_space=pl.ANY)
VMEM = pl.BlockSpec(memory_space=pltpu.VMEM)


def place(n_col):
    me = lax.axis_index("col")
    far, mid, core = me // 4, lax.rem(me // 2, 2), lax.rem(me, 2)
    return me, far, mid, core, lambda f, m, c: (f * 2 + m) * 2 + c


def greet(cols, orbs):
    barrier = pltpu.get_barrier_semaphore()
    for col in cols:
        pl.semaphore_signal(barrier, inc=1, device_id={"col": col}, device_id_type=MESH)
    for orb in orbs:
        pl.semaphore_signal(barrier, inc=1, device_id={"orb": orb}, device_id_type=MESH)
    pl.semaphore_wait(barrier, len(cols) + len(orbs))


def gather_kernel(
    n_col, slab, occ, vir, screen, slabs, peer_occ, peer_vir, screens,
    local_sem, orb_send, orb_recv, slab_send, slab_recv, screen_send, screen_recv,
):
    n_far = n_col // 4
    me, far, mid, core, index = place(n_col)
    part = lax.axis_index("orb")
    other = 1 - part
    others = [lax.rem(me + d, n_col) for d in range(1, n_col)]
    greet(others, [other])

    sends = []

    def push(src, dst, send, recv, device):
        copy = pltpu.make_async_remote_copy(
            src_ref=src, dst_ref=dst, send_sem=send, recv_sem=recv,
            device_id=device, device_id_type=MESH,
        )
        copy.start()
        sends.append(copy)

    push(slab.at[other], slabs.at[1, me], orb_send.at[2], slab_recv.at[1, me], {"orb": other})
    push(vir, peer_vir, orb_send.at[0], orb_recv.at[0], {"orb": other})
    push(occ, peer_occ, orb_send.at[1], orb_recv.at[1], {"orb": other})

    def arrived(k, col):
        ref = slabs.at[k, col]
        pltpu.make_async_remote_copy(
            src_ref=ref, dst_ref=ref, send_sem=orb_send.at[2], recv_sem=slab_recv.at[k, col],
            device_id={"orb": other}, device_id_type=MESH,
        ).wait_recv()

    counter = [0]

    def give(k, col, target, src=None):
        push(
            slabs.at[k, col] if src is None else src, slabs.at[k, col],
            slab_send.at[counter[0]], slab_recv.at[k, col], {"col": target},
        )
        counter[0] += 1

    x_peer, core_peer = index(far, 1 - mid, core), index(far, mid, 1 - core)
    fars = [lax.rem(far + d, n_far) for d in range(1, n_far)]
    own = slab.at[part]
    targets = [index(f, mid, core) for f in fars] + [x_peer, core_peer]
    for target in targets:
        give(0, me, target, own)
    arrived(1, me)
    for target in targets:
        give(1, me, target)
    for n, p in enumerate(others):
        push(screen.at[p], screens.at[me], screen_send.at[n], screen_recv.at[me], {"col": p})
    local = [
        pltpu.make_async_copy(own, slabs.at[0, me], local_sem.at[0]),
        pltpu.make_async_copy(screen.at[me], screens.at[me], local_sem.at[1]),
    ]
    for copy in local:
        copy.start()
    for f in fars:
        col = index(f, mid, core)
        for k in range(2):
            arrived(k, col)
            give(k, col, x_peer)
            give(k, col, core_peer)
    for f in [far] + fars:
        col = index(f, 1 - mid, core)
        for k in range(2):
            arrived(k, col)
            give(k, col, core_peer)
    for f in [far] + fars:
        for m in (mid, 1 - mid):
            for k in range(2):
                arrived(k, index(f, m, 1 - core))
    for p in others:
        ref = screens.at[p]
        pltpu.make_async_remote_copy(
            src_ref=ref, dst_ref=ref, send_sem=orb_send.at[2], recv_sem=screen_recv.at[p],
            device_id={"orb": other}, device_id_type=MESH,
        ).wait_recv()
    for n, ref in ((0, peer_vir), (1, peer_occ)):
        pltpu.make_async_remote_copy(
            src_ref=ref, dst_ref=ref, send_sem=orb_send.at[n], recv_sem=orb_recv.at[n],
            device_id={"orb": other}, device_id_type=MESH,
        ).wait_recv()
    for copy in local:
        copy.wait()
    for copy in sends:
        copy.wait_send()


def gather(n_col, slab, occ, vir, screen):
    n_far = n_col // 4
    dma = pltpu.SemaphoreType.DMA
    n_give = 2 * ((n_far + 1) + 2 * (n_far - 1) + n_far)
    return pl.pallas_call(
        functools.partial(gather_kernel, n_col),
        out_shape=(
            jax.ShapeDtypeStruct((2, n_col) + slab.shape[1:], slab.dtype),
            jax.ShapeDtypeStruct(occ.shape, occ.dtype),
            jax.ShapeDtypeStruct(vir.shape, vir.dtype),
            jax.ShapeDtypeStruct(screen.shape, screen.dtype),
        ),
        in_specs=[ANY] * 4,
        out_specs=(ANY,) * 4,
        scratch_shapes=[
            dma((2,)), dma((3,)), dma((2,)), dma((n_give,)), dma((2, n_col)),
            dma((n_col,)), dma((n_col,)),
        ],
        compiler_params=pltpu.CompilerParams(collective_id=0, has_side_effects=True),
    )(slab, occ, vir, screen)


def scatter_kernel(n_col, pieces, *refs):
    n_far = n_col // 4
    ins, refs = refs[:pieces], refs[pieces:]
    outs, refs = refs[:pieces], refs[pieces:]
    near, out_x, in_x, total, out_far, in_far = [
        refs[i * pieces : (i + 1) * pieces] for i in range(6)
    ]
    near_send, near_recv, x_send, x_recv, far_send, far_recv = refs[6 * pieces :]
    me, far, mid, core, index = place(n_col)
    x_peer, core_peer = index(far, 1 - mid, core), index(far, mid, 1 - core)
    fars = [lax.rem(far + d, n_far) for d in range(1, n_far)]
    greet([core_peer, x_peer] + [index(f, mid, core) for f in fars], [])

    def copy(src, dst, send, recv, target):
        made = pltpu.make_async_remote_copy(
            src_ref=src, dst_ref=dst, send_sem=send, recv_sem=recv,
            device_id={"col": target}, device_id_type=MESH,
        )
        made.start()
        return made

    wide = lambda value: value.astype(jnp.float32)
    first = [[None, None] for t in range(pieces)]
    for t in range(pieces):
        for slot, m in ((0, 1 - mid), (1, mid)):
            first[t][slot] = copy(
                ins[t].at[:, m, 1 - core], near[t].at[slot],
                near_send.at[t, slot], near_recv.at[t, slot], core_peer,
            )
    second = []
    for t in range(pieces):
        first[t][0].wait_recv()
        for f in range(n_far):
            out_x[t][f] = (wide(ins[t][f, 1 - mid, core]) + wide(near[t][0, f])).astype(
                out_x[t].dtype
            )
        second.append(copy(out_x[t], in_x[t], x_send.at[t], x_recv.at[t], x_peer))
        first[t][1].wait_recv()
        for f in range(n_far):
            total[t][f] = wide(ins[t][f, mid, core]) + wide(near[t][1, f])
    third = []
    for t in range(pieces):
        second[t].wait_recv()
        for f in range(n_far):
            total[t][f] = total[t][f] + wide(in_x[t][f])
            out_far[t][f] = total[t][f].astype(out_far[t].dtype)
        for d, f in enumerate(fars):
            third.append(
                copy(
                    out_far[t].at[f], in_far[t].at[d],
                    far_send.at[t, d], far_recv.at[t, d], index(f, mid, core),
                )
            )
    for t in range(pieces):
        value = total[t][far]
        for d in range(n_far - 1):
            third[t * (n_far - 1) + d].wait_recv()
            value = value + wide(in_far[t][d])
        outs[t][...] = value.astype(outs[t].dtype)
    for made in sum(first, []) + second + third:
        made.wait_send()


def scatter(n_col, terms):
    n_far = n_col // 4
    dma = pltpu.SemaphoreType.DMA
    pieces = len(terms)
    block, kind = [t.shape[-2:] for t in terms], terms[0].dtype

    def buffers(lead, dtype=kind):
        return [pltpu.VMEM(lead + b, dtype) for b in block]

    return pl.pallas_call(
        functools.partial(scatter_kernel, n_col, pieces),
        out_shape=[jax.ShapeDtypeStruct(b, kind) for b in block],
        in_specs=[VMEM] * pieces,
        out_specs=[VMEM] * pieces,
        scratch_shapes=buffers((2, n_far))
        + buffers((n_far,))
        + buffers((n_far,))
        + buffers((n_far,), jnp.float32)
        + buffers((n_far,))
        + buffers((n_far - 1,))
        + [
            dma((pieces, 2)), dma((pieces, 2)), dma((pieces,)), dma((pieces,)),
            dma((pieces, n_far - 1)), dma((pieces, n_far - 1)),
        ],
        compiler_params=pltpu.CompilerParams(collective_id=1, has_side_effects=True),
    )(*terms)


def local(slab_occ, slab_vir, orbitals_occ, orbitals_vir, occ_energy, vir_energy, screened):
    n_orb, n_col = lax.axis_size("orb"), lax.axis_size("col")
    part = lax.axis_index("orb")
    block = slab_occ.shape[0] // n_orb
    n_occ, columns = orbitals_occ.shape
    n_vir = orbitals_vir.shape[0]
    kind = slab_occ.dtype
    up = lambda n: -(-n // 128) * 128
    scaled_occ = (slab_occ.astype(jnp.float32) * jnp.exp(occ_energy)[None, :]).astype(kind)
    scaled_vir = (slab_vir.astype(jnp.float32) * jnp.exp(-vir_energy)[None, :]).astype(kind)
    start = up(n_vir)
    slab = jnp.concatenate(
        [
            jnp.pad(scaled_vir, ((0, 0), (0, start - n_vir))),
            jnp.pad(scaled_occ, ((0, 0), (0, up(n_occ) - n_occ))),
        ],
        axis=1,
    ).reshape((n_orb, block, start + up(n_occ)))
    mine = lax.dynamic_slice_in_dim(screened, part * block, block, 0)
    mine = mine.reshape((block, n_col, columns)).transpose((1, 0, 2))
    slabs, peer_occ, peer_vir, screens = gather(n_col, slab, orbitals_occ, orbitals_vir, mine)
    slabs = slabs.reshape((2, n_col * block, slab.shape[2]))
    own_slab, peer_slab = slabs[0], slabs[1]

    def dot(a, b):
        return jnp.dot(a, b, preferred_element_type=jnp.float32)

    green_vir = dot(own_slab[:, :n_vir], orbitals_vir) + dot(peer_slab[:, :n_vir], peer_vir)
    green_occ = dot(own_slab[:, start : start + n_occ], orbitals_occ) + dot(
        peer_slab[:, start : start + n_occ], peer_occ
    )
    screen = screens.reshape((n_col * block, columns)).astype(jnp.float32)
    occ_side = (green_vir * screen).astype(kind)
    vir_side = (green_occ * screen).astype(kind)
    dims = (((1,), (1,)), ((), ()))

    def project(side, orbitals):
        term = lax.dot_general(side, orbitals, dims, preferred_element_type=jnp.float32)
        return term.astype(kind).reshape((n_col // 4, 2, 2, block, orbitals.shape[0]))

    vir_own, vir_peer, occ_own, occ_peer = scatter(
        n_col,
        [
            project(vir_side, orbitals_vir),
            project(vir_side, peer_vir),
            project(occ_side, orbitals_occ),
            project(occ_side, peer_occ),
        ],
    )

    def order(own, peer):
        return jnp.where(
            part == 0, jnp.concatenate([own, peer], 1), jnp.concatenate([peer, own], 1)
        )

    return order(occ_own, occ_peer), order(vir_own, vir_peer)


def solution(mesh):
    return jax.shard_map(
        local,
        mesh=mesh,
        in_specs=(
            P("col", "orb"),
            P("col", "orb"),
            P("orb", "col"),
            P("orb", "col"),
            P("orb"),
            P("orb"),
            P("col", None),
        ),
        out_specs=(P(("col", "orb"), None), P(("col", "orb"), None)),
        check_vma=False,
    )
```
